1024 devices in a mesh: dp: 256 (over z, y, core), gz: 4 (over x).
Axes of the slice: x: 4, y: 8, z: 16, core: 2. Of those that a mesh axis runs over, the one named last changes fastest.
Arguments:
- features_in: bfloat16 [256, 32, 16, 512], P('dp', None, 'gz'), may hold values from -6 to 6
- kernel_taps: bfloat16 [27, 2048], replicated, may hold values from -0.21875 to 0.21875
- channel_bias: float32 [64], replicated, may hold values from -3 to 3
- upstream: bfloat16 [256, 64, 16, 512], P('dp', None, 'gz'), may hold values from -6 to 6
Outputs:
- output: bfloat16 [256, 64, 16, 512], P('dp', None, 'gz')
- grad_input: bfloat16 [256, 32, 16, 512], P('dp', None, 'gz')
- weight_grad: float32 [27, 2048], replicated
- bias_grad: float32 [64], replicated
The draws below stay inside these ranges and needn't reach their ends.
All inputs are finite; a program needn't handle non-finite values.
Results may differ from the reference program's by a relative error of at most 0.0034.
Values may be sent and summed in bfloat16 or wider, within the bound.
No kernel may reach another device: no remote copies, remote signals or barrier semaphores. Data moves between devices by JAX's collectives and lax.ppermute only.
A program may use at most 32 MiB of HBM per device.

```python
import math
import jax
import jax.numpy as jnp
from jax import lax

CIN = 32
COUT = 64
NX = 64
NY = 8
VOLUMES = 256
NZ = 16


def shard_levels(stream_key, extent, shards, low, high):
    level, own = 1.0, jax.random.fold_in(stream_key, 6)
    for axis_at, blocks in shards:
        draws = jnp.exp(jax.random.uniform(jax.random.fold_in(own, axis_at), (blocks,), jnp.float32, low / len(shards), high / len(shards)))
        level = level * jnp.repeat(draws, extent[axis_at] // blocks).reshape([-1 if axis == axis_at else 1 for axis in range(len(extent))])
    return level


def centred(key, shape, spread, bound, pieces=(), kind=jnp.bfloat16):
    array = jax.random.normal(key, shape, jnp.float32) * spread
    if len(pieces) > 0:
        array = shard_levels(key, shape, pieces, -0.22, 0.18) * array
    return jnp.clip(array, min=-bound, max=bound).astype(kind)


def setup_inputs(seed: int = 0) -> dict:
    arg_keys = jax.random.split(jax.random.key(seed), 5)
    features_in = centred(arg_keys[0], (VOLUMES, CIN, NZ, NY * NX), 1.0, 6.0, ((0, 256), (2, 4)))
    kernel_taps = centred(arg_keys[1], (27, CIN * COUT), (27 * CIN) ** -0.5, 0.21875)
    channel_bias = centred(arg_keys[2], (COUT,), 0.5, 3.0, (), jnp.float32)
    upstream = centred(arg_keys[3], (VOLUMES, COUT, NZ, NY * NX), 1.0, 6.0, ((0, 256), (2, 4)))
    return {"features_in": features_in, "kernel_taps": kernel_taps, "channel_bias": channel_bias, "upstream": upstream}


def correlate(field, taps):
    return lax.conv_general_dilated(field, taps, (1, 1, 1), 'VALID', dimension_numbers=('NCDHW', 'DHWIO', 'NCDHW'), precision=lax.Precision.HIGHEST)

def reference(features_in, kernel_taps, channel_bias, upstream):
    kernel = kernel_taps.astype(jnp.float32).reshape(3, 3, 3, CIN, COUT)
    flipped = jnp.transpose(kernel[::-1, ::-1, ::-1], (0, 1, 2, 4, 3))
    widths = ((0, 0), (0, 0), (1, 1), (1, 1), (1, 1))
    feats = features_in.reshape(VOLUMES, CIN, NZ, NY, NX)
    grads = upstream.reshape(VOLUMES, COUT, NZ, NY, NX)

    def one_volume(carry, pair):
        field, grad = pair
        padded_in = jnp.pad(field.astype(jnp.float32)[None], widths)
        grad_whole = grad.astype(jnp.float32)[None]
        padded_up = jnp.pad(grad_whole, widths)
        result = correlate(padded_in, kernel) + channel_bias.astype(jnp.float32)[None, :, None, None, None]
        back = correlate(padded_up, flipped)
        weight_term = lax.conv_general_dilated(padded_in, grad_whole, (1, 1, 1), 'VALID', dimension_numbers=('CNDHW', 'IODHW', 'DHWNC'), precision=lax.Precision.HIGHEST)
        weight_term = weight_term.reshape(27, CIN * COUT)
        bias_term = lax.optimization_barrier(jnp.sum(grad_whole, axis=(0, 2, 3, 4)))
        return ((carry[0] + weight_term, carry[1] + bias_term), (result[0].astype(jnp.bfloat16), back[0].astype(jnp.bfloat16)))
    start = (jnp.zeros((27, CIN * COUT), jnp.float32), jnp.zeros((COUT,), jnp.float32))
    totals, results = lax.scan(one_volume, start, (feats, grads))
    factor = 1.0 / math.sqrt(VOLUMES * NZ * NY * NX)
    out_main = results[0].reshape(VOLUMES, COUT, NZ, NY * NX)
    out_back = results[1].reshape(VOLUMES, CIN, NZ, NY * NX)
    return (out_main, out_back, totals[0] * factor, totals[1] * factor)
```

```python
import math

import jax
import jax.numpy as jnp
from jax import lax
from jax.sharding import Mesh
from jax.sharding import PartitionSpec as P

NX = 64
NY = 8
DP = ("dp_0", "dp_1", "dp_2")


def with_halo(cells, sides, width):
    for axis, dim in sides:
        count = lax.axis_size(axis)
        ends = count - 1
        head = lax.slice_in_dim(cells, 0, width, axis=dim)
        tail = lax.slice_in_dim(cells, cells.shape[dim] - width, cells.shape[dim], axis=dim)
        cells = jnp.concatenate(
            [
                lax.ppermute(tail, axis, [(i, (i + 1) % count) for i in range(ends)]),
                cells,
                lax.ppermute(head, axis, [((i + 1) % count, i) for i in range(ends)]),
            ],
            axis=dim,
        )
    return cells


TILES = 64
NEAR = ("dp_1", "dp_2", "gz")


def swap(blocks, axes):
    return lax.all_to_all(blocks, axes, 0, 0, tiled=True)


def sum_everywhere(tiles):
    own = jnp.sum(swap(tiles, NEAR), axis=0)
    far = lax.axis_size("dp_0")
    own = jnp.sum(swap(jnp.broadcast_to(own, (far, *own.shape)), "dp_0"), axis=0)
    return swap(jnp.broadcast_to(own, tiles.shape), NEAR)


def pad_sides(field):
    return jnp.pad(field, ((0, 0), (0, 0), (0, 0), (1, 1), (1, 1)))


def correlate(field, taps):
    return lax.conv_general_dilated(
        field,
        taps,
        (1, 1, 1),
        "VALID",
        dimension_numbers=("NCDHW", "DHWIO", "NCDHW"),
        preferred_element_type=jnp.float32,
    )


def on_device(features_in, kernel_taps, channel_bias, upstream):
    in_chan = features_in.shape[1]
    out_chan = upstream.shape[1]
    vol_count = features_in.shape[0]
    planes = features_in.shape[2]
    kernel = kernel_taps.reshape(3, 3, 3, in_chan, out_chan)
    flipped = jnp.transpose(kernel[::-1, ::-1, ::-1], (0, 1, 2, 4, 3))
    feats = features_in.reshape(vol_count, in_chan, planes, NY, NX)
    grads = upstream.reshape(vol_count, out_chan, planes, NY, NX)
    padded_in = pad_sides(with_halo(feats, (("gz", 2),), 1))
    padded_up = pad_sides(with_halo(grads, (("gz", 2),), 1))
    output = (correlate(padded_in, kernel) + channel_bias[None, :, None, None, None]).astype(
        jnp.bfloat16
    )
    grad_input = correlate(padded_up, flipped).astype(jnp.bfloat16)
    weight_term = lax.conv_general_dilated(
        padded_in,
        grads,
        (1, 1, 1),
        "VALID",
        dimension_numbers=("CNDHW", "IODHW", "DHWNC"),
        preferred_element_type=jnp.float32,
    )
    weight_term = weight_term.reshape(27, in_chan * out_chan)
    bias_term = jnp.sum(grads, axis=(0, 2, 3, 4), dtype=jnp.float32)
    cells_all = vol_count * lax.axis_size(DP) * planes * lax.axis_size("gz") * NY * NX
    factor = 1.0 / math.sqrt(cells_all)
    rows = jnp.concatenate([weight_term, jnp.pad(bias_term[None], ((0, 4), (0, 2048 - out_chan)))])
    tiles = rows.reshape(4, 8, 16, 128).transpose(0, 2, 1, 3).reshape(TILES, 8, 128)
    total = sum_everywhere(tiles)
    total = total.reshape(4, 16, 8, 128).transpose(0, 2, 1, 3).reshape(32, 2048)
    weight_sum, bias_sum = (total[:27], total[27, :out_chan])
    output = output.reshape(vol_count, out_chan, planes, NY * NX)
    grad_input = grad_input.reshape(vol_count, in_chan, planes, NY * NX)
    return (output, grad_input, weight_sum * factor, bias_sum * factor)


def solution(mesh):
    split = Mesh(mesh.devices.reshape(16, 8, 2, mesh.shape["gz"]), ("dp_0", "dp_1", "dp_2", "gz"))
    placed = (P(DP, None, "gz", None), P(), P(), P(DP, None, "gz", None))
    return jax.shard_map(
        on_device,
        mesh=split,
        in_specs=placed,
        out_specs=(P(DP, None, "gz", None), P(DP, None, "gz", None), P(), P()),
        check_vma=False,
    )
```

```python
import functools
import math

import jax
import jax.numpy as jnp
from jax import lax
from jax.experimental import pallas as pl
from jax.experimental.pallas import tpu as pltpu
from jax.sharding import Mesh
from jax.sharding import PartitionSpec as P

NX = 64
NY = 8
DP = ("dp_0", "dp_1", "dp_2")
NEAR = ("dp_1", "dp_2", "gz")
TILES = 64
ROWS = 32
INTERPRET = False
VMEM = pl.BlockSpec(memory_space=pltpu.VMEM)


def on_core(body, out_shape, scratch=()):
    return pl.pallas_call(
        body,
        out_shape=out_shape,
        scratch_shapes=list(scratch),
        interpret=INTERPRET,
    )


def inside(width, db, dc):
    lane = lax.broadcasted_iota(jnp.int32, (1, width), 1)
    x = (lane & (NX - 1)) + dc
    y = lax.shift_right_logical(lane, NX.bit_length() - 1) + db
    return (x >= 0) & (x < NX) & (y >= 0) & (y < NY)


def moved(plane, b, c):
    width = plane.shape[-1]
    off = (b - 1) * NX + c - 1
    if off == 0:
        return plane
    return jnp.where(inside(width, b - 1, c - 1), pltpu.roll(plane, (-off) % width, 1), 0.0)


def store_moved(s_ref, at, plane):
    plane = plane.astype(jnp.float32)
    chans = plane.shape[0]
    for b in range(3):
        for c in range(3):
            row = at + (3 * b + c) * chans
            s_ref[row : row + chans, :] = moved(plane, b, c).astype(jnp.bfloat16)


def split_body(f_ref, u_ref, head_ref, mid_ref, tail_ref):
    cin, planes, _ = f_ref.shape
    for ref, at in ((f_ref, 0), (u_ref, cin)):
        rows = slice(at, at + ref.shape[0])
        own = jnp.swapaxes(ref[...].astype(jnp.float32), 0, 1).astype(jnp.bfloat16)
        head_ref[rows, :] = own[0]
        tail_ref[rows, :] = own[planes - 1]
        for z in range(1, planes - 1):
            mid_ref[z - 1, rows, :] = own[z]


def planes_of(head_ref, mid_ref, tail_ref, rows):
    mid = [mid_ref[z, rows, :] for z in range(mid_ref.shape[0])]
    return [head_ref[rows, :], *mid, tail_ref[rows, :]]


NT = (((1,), (1,)), ((), ()))


def dot(a, b, dims=(((1,), (0,)), ((), ()))):
    return lax.dot_general(a, b, dims, preferred_element_type=jnp.float32)


def own_body(cin, head_ref, mid_ref, tail_ref, w_ref, s_ref):
    width = head_ref.shape[1]
    cout = head_ref.shape[0] - cin
    taps = 9 * cin
    own = planes_of(head_ref, mid_ref, tail_ref, slice(0, cin))
    ups = planes_of(head_ref, mid_ref, tail_ref, slice(cin, cin + cout))
    planes = len(own)
    for z in range(planes):
        store_moved(s_ref, z * taps, own[z])
    twice = [jnp.concatenate([up, up], axis=0) for up in ups]
    for a in range(3):
        total = jnp.zeros((taps, 2 * cout), jnp.float32)
        for z in range(planes):
            src = z + a - 1
            if 0 <= src < planes:
                total += dot(s_ref[src * taps : (src + 1) * taps, :], twice[z], NT)
        w_ref[a * taps : (a + 1) * taps, :] = total
    ones = jnp.ones((16, width), jnp.bfloat16)
    bias = jnp.zeros((16, 2 * cout), jnp.float32)
    for z in range(planes):
        bias += dot(ones, twice[z], NT)
    w_ref[3 * taps :, :] = jnp.zeros((w_ref.shape[0] - 3 * taps, 2 * cout), jnp.float32)
    w_ref[3 * taps : 3 * taps + 8, :] = bias[:8]


def edge_body(cin, factor, lo_ref, head_ref, tail_ref, hi_ref, w_ref, tiles_ref, s_ref, v_ref):
    cout = lo_ref.shape[0] - cin
    taps = 9 * cin
    v_ref[...] = w_ref[...]
    for a, there_ref, here_ref in ((0, lo_ref, head_ref), (2, hi_ref, tail_ref)):
        at = a // 2 * taps
        store_moved(s_ref, at, there_ref[:cin, :])
        up = here_ref[cin:, :]
        twice = jnp.concatenate([up, up], axis=0)
        v_ref[a * taps : (a + 1) * taps, :] += dot(s_ref[at : at + taps, :], twice, NT)
    left = lax.broadcasted_iota(jnp.int32, (ROWS, 2 * cout), 1) < cout
    for at in range(cin // 2):
        even = v_ref[pl.ds(2 * at, ROWS, stride=cin), :]
        odd = v_ref[pl.ds(2 * at + 1, ROWS, stride=cin), :]
        tiles_ref[:, at] = (jnp.where(left, even, odd) * factor).reshape(ROWS // 8, 8, 2 * cout)


def forward_body(cin, lo_ref, head_ref, mid_ref, tail_ref, hi_ref, w_ref, bias_ref, out_ref, s_ref):
    taps = 9 * cin
    rows = slice(0, cin)
    slabs = [lo_ref[rows, :], *planes_of(head_ref, mid_ref, tail_ref, rows), hi_ref[rows, :]]
    for z, plane in enumerate(slabs):
        store_moved(s_ref, z * taps, plane)
    outs = [dot(w_ref[...], s_ref[z * taps : (z + 3) * taps, :]) + bias_ref[...] for z in range(len(slabs) - 2)]
    out_ref[...] = jnp.swapaxes(jnp.stack(outs), 0, 1).astype(jnp.bfloat16)


def backward_body(cin, lo_ref, head_ref, mid_ref, tail_ref, hi_ref, w_ref, _, out_ref, p_ref):
    width = lo_ref.shape[1]
    cout = lo_ref.shape[0] - cin
    rows = slice(cin, cin + cout)
    slabs = [lo_ref[rows, :], *planes_of(head_ref, mid_ref, tail_ref, rows), hi_ref[rows, :]]
    for z, plane in enumerate(slabs):
        p_ref[z * cout : (z + 1) * cout, :] = plane
    outs = []
    for z in range(len(slabs) - 2):
        parts = dot(w_ref[...], p_ref[z * cout : (z + 3) * cout, :])
        total = jnp.zeros((cin, width), jnp.float32)
        for b in range(3):
            for c in range(3):
                at = (3 * b + c) * cin
                total += moved(parts[at : at + cin], b, c)
        outs.append(total)
    out_ref[...] = jnp.swapaxes(jnp.stack(outs), 0, 1).astype(jnp.bfloat16)


def split_planes(feats, grads):
    planes, width = feats.shape[1:]
    rows = feats.shape[0] + grads.shape[0]
    one = jax.ShapeDtypeStruct((rows, width), feats.dtype)
    return on_core(split_body, (one, jax.ShapeDtypeStruct((planes - 2, rows, width), feats.dtype), one))(feats, grads)


def own_terms(cin, head, mid, tail):
    rows, width = head.shape
    planes = mid.shape[0] + 2
    return on_core(
        functools.partial(own_body, cin),
        jax.ShapeDtypeStruct((ROWS * cin, 2 * (rows - cin)), jnp.float32),
        [pltpu.VMEM((planes * 9 * cin, width), jnp.bfloat16)],
    )(head, mid, tail)


def weight_tiles(cin, lo, head, tail, hi, own, factor):
    rows, width = lo.shape
    return on_core(
        functools.partial(edge_body, cin, factor),
        jax.ShapeDtypeStruct((ROWS // 8, cin // 2, 8, 2 * (rows - cin)), jnp.float32),
        [pltpu.VMEM((18 * cin, width), jnp.bfloat16), pltpu.VMEM(own.shape, jnp.float32)],
    )(lo, head, tail, hi, own)


def forward(cin, slabs, taps, bias):
    rows, width = slabs[0].shape
    planes = slabs[2].shape[0] + 2
    return on_core(
        functools.partial(forward_body, cin),
        jax.ShapeDtypeStruct((rows - cin, planes, width), jnp.bfloat16),
        [pltpu.VMEM(((planes + 2) * 9 * cin, width), jnp.bfloat16)],
    )(*slabs, taps, bias)


def backward(cin, slabs, taps, after):
    rows, width = slabs[0].shape
    planes = slabs[2].shape[0] + 2
    return on_core(
        functools.partial(backward_body, cin),
        jax.ShapeDtypeStruct((cin, planes, width), jnp.bfloat16),
        [pltpu.VMEM(((planes + 2) * (rows - cin), width), jnp.bfloat16)],
    )(*slabs, taps, after)


def swap(blocks, axes):
    return lax.all_to_all(blocks, axes, 0, 0, tiled=True)


def on_device(features_in, kernel_taps, channel_bias, upstream):
    feats, grads = features_in[0], upstream[0]
    cin, depth, width = feats.shape
    cout = grads.shape[0]
    cells_all = lax.axis_size(DP) * depth * lax.axis_size("gz") * width
    factor = 1.0 / math.sqrt(cells_all)
    head, mid, tail = split_planes(feats, grads)
    slabs = lax.axis_size("gz")
    lo = lax.ppermute(tail, "gz", [(i, i + 1) for i in range(slabs - 1)])
    hi = lax.ppermute(head, "gz", [(i + 1, i) for i in range(slabs - 1)])
    planes = (lo, head, mid, tail, hi)
    kernel = kernel_taps.reshape(27, cin, cout)
    ahead = kernel.reshape(27 * cin, cout).T
    back = kernel[::-1].reshape(3, 9, cin, cout).transpose(1, 2, 0, 3).reshape(9 * cin, 3 * cout)
    own = own_terms(cin, head, mid, tail)
    tiles = weight_tiles(cin, lo, head, tail, hi, own, factor).reshape(TILES, 8, 128)
    part = jnp.sum(swap(tiles, NEAR), axis=0)
    output = forward(cin, planes, ahead, channel_bias[:, None])
    part, output = lax.optimization_barrier((part, output))
    grad_input = backward(cin, planes, back, part)
    far = lax.axis_size("dp_0")
    part = jnp.sum(swap(jnp.broadcast_to(part, (far, *part.shape)), "dp_0"), axis=0)
    part, grad_input = lax.optimization_barrier((part, grad_input))
    total = swap(jnp.broadcast_to(part, tiles.shape), NEAR)
    total = total.reshape(4, 16, 8, 128).transpose(0, 2, 1, 3).reshape(ROWS, 2048)
    return (output[None], grad_input[None], total[:27], total[27, :cout])


def solution(mesh):
    split = Mesh(mesh.devices.reshape(16, 8, 2, mesh.shape["gz"]), ("dp_0", "dp_1", "dp_2", "gz"))
    placed = (P(DP, None, "gz", None), P(), P(), P(DP, None, "gz", None))
    return jax.shard_map(
        on_device,
        mesh=split,
        in_specs=placed,
        out_specs=(P(DP, None, "gz", None), P(DP, None, "gz", None), P(), P()),
        check_vma=False,
    )
```

```python
import functools
import math

import jax
import jax.numpy as jnp
from jax import lax
from jax.experimental import pallas as pl
from jax.experimental.pallas import tpu as pltpu
from jax.sharding import Mesh
from jax.sharding import PartitionSpec as P

NX = 64
NY = 8
DP = ("dp_0", "dp_1", "dp_2")
NEAR = ("dp_1", "dp_2", "gz")
TILES = 64
ROWS = 32
INTERPRET = False
VMEM = pl.BlockSpec(memory_space=pltpu.VMEM)


def on_core(body, out_shape, scratch=(), held=True, near=True):
    def call(*operands):
        if held:
            operands = [pltpu.with_memory_space_constraint(x, pltpu.VMEM) for x in operands]
        return pl.pallas_call(
            body,
            out_shape=jax.tree.map(lambda s: pltpu.VMEM(s.shape, s.dtype), out_shape) if near else out_shape,
            in_specs=[VMEM] * len(operands),
            out_specs=jax.tree.map(lambda _: VMEM, out_shape),
            scratch_shapes=list(scratch),
            interpret=INTERPRET,
        )(*operands)

    return call


def inside(width, db, dc):
    lane = lax.broadcasted_iota(jnp.int32, (1, width), 1)
    x = (lane & (NX - 1)) + dc
    y = lax.shift_right_logical(lane, NX.bit_length() - 1) + db
    return (x >= 0) & (x < NX) & (y >= 0) & (y < NY)


def moved(plane, b, c):
    width = plane.shape[-1]
    off = (b - 1) * NX + c - 1
    if off == 0:
        return plane
    return jnp.where(inside(width, b - 1, c - 1), pltpu.roll(plane, (-off) % width, 1), 0.0)


def store_moved(s_ref, at, plane):
    plane = plane.astype(jnp.float32)
    chans = plane.shape[0]
    for b in range(3):
        for c in range(3):
            row = at + (3 * b + c) * chans
            s_ref[row : row + chans, :] = moved(plane, b, c).astype(jnp.bfloat16)


def split_body(f_ref, u_ref, head_ref, mid_ref, tail_ref):
    cin, planes, _ = f_ref.shape
    for ref, at in ((f_ref, 0), (u_ref, cin)):
        rows = slice(at, at + ref.shape[0])
        own = jnp.swapaxes(ref[...].astype(jnp.float32), 0, 1).astype(jnp.bfloat16)
        head_ref[rows, :] = own[0]
        tail_ref[rows, :] = own[planes - 1]
        for z in range(1, planes - 1):
            mid_ref[z - 1, rows, :] = own[z]


def planes_of(head_ref, mid_ref, tail_ref, rows):
    mid = [mid_ref[z, rows, :] for z in range(mid_ref.shape[0])]
    return [head_ref[rows, :], *mid, tail_ref[rows, :]]


NT = (((1,), (1,)), ((), ()))


def dot(a, b, dims=(((1,), (0,)), ((), ()))):
    return lax.dot_general(a, b, dims, preferred_element_type=jnp.float32)


def own_body(cin, head_ref, mid_ref, tail_ref, w_ref, s_ref):
    width = head_ref.shape[1]
    cout = head_ref.shape[0] - cin
    taps = 9 * cin
    own = planes_of(head_ref, mid_ref, tail_ref, slice(0, cin))
    ups = planes_of(head_ref, mid_ref, tail_ref, slice(cin, cin + cout))
    planes = len(own)
    for z in range(planes):
        store_moved(s_ref, z * taps, own[z])
    twice = [jnp.concatenate([up, up], axis=0) for up in ups]
    for a in range(3):
        total = jnp.zeros((taps, 2 * cout), jnp.float32)
        for z in range(planes):
            src = z + a - 1
            if 0 <= src < planes:
                total += dot(s_ref[src * taps : (src + 1) * taps, :], twice[z], NT)
        w_ref[a * taps : (a + 1) * taps, :] = total
    ones = jnp.ones((16, width), jnp.bfloat16)
    bias = jnp.zeros((16, 2 * cout), jnp.float32)
    for z in range(planes):
        bias += dot(ones, twice[z], NT)
    w_ref[3 * taps :, :] = jnp.zeros((w_ref.shape[0] - 3 * taps, 2 * cout), jnp.float32)
    w_ref[3 * taps : 3 * taps + 8, :] = bias[:8]


def edge_body(cin, factor, lo_ref, head_ref, tail_ref, hi_ref, w_ref, tiles_ref, s_ref, v_ref):
    cout = lo_ref.shape[0] - cin
    taps = 9 * cin
    v_ref[...] = w_ref[...]
    for a, there_ref, here_ref in ((0, lo_ref, head_ref), (2, hi_ref, tail_ref)):
        at = a // 2 * taps
        store_moved(s_ref, at, there_ref[:cin, :])
        up = here_ref[cin:, :]
        twice = jnp.concatenate([up, up], axis=0)
        v_ref[a * taps : (a + 1) * taps, :] += dot(s_ref[at : at + taps, :], twice, NT)
    left = lax.broadcasted_iota(jnp.int32, (ROWS, 2 * cout), 1) < cout
    for at in range(cin // 2):
        even = v_ref[pl.ds(2 * at, ROWS, stride=cin), :]
        odd = v_ref[pl.ds(2 * at + 1, ROWS, stride=cin), :]
        tiles_ref[:, at] = (jnp.where(left, even, odd) * factor).reshape(ROWS // 8, 8, 2 * cout)


def forward_body(cin, lo_ref, head_ref, mid_ref, tail_ref, hi_ref, w_ref, bias_ref, out_ref, s_ref):
    taps = 9 * cin
    rows = slice(0, cin)
    slabs = [lo_ref[rows, :], *planes_of(head_ref, mid_ref, tail_ref, rows), hi_ref[rows, :]]
    for z, plane in enumerate(slabs):
        store_moved(s_ref, z * taps, plane)
    outs = [dot(w_ref[...], s_ref[z * taps : (z + 3) * taps, :]) + bias_ref[...] for z in range(len(slabs) - 2)]
    out_ref[...] = jnp.swapaxes(jnp.stack(outs), 0, 1).astype(jnp.bfloat16)


def backward_body(cin, lo_ref, head_ref, mid_ref, tail_ref, hi_ref, w_ref, _, out_ref, p_ref):
    width = lo_ref.shape[1]
    cout = lo_ref.shape[0] - cin
    rows = slice(cin, cin + cout)
    slabs = [lo_ref[rows, :], *planes_of(head_ref, mid_ref, tail_ref, rows), hi_ref[rows, :]]
    for z, plane in enumerate(slabs):
        p_ref[z * cout : (z + 1) * cout, :] = plane
    outs = []
    for z in range(len(slabs) - 2):
        parts = dot(w_ref[...], p_ref[z * cout : (z + 3) * cout, :])
        total = jnp.zeros((cin, width), jnp.float32)
        for b in range(3):
            for c in range(3):
                at = (3 * b + c) * cin
                total += moved(parts[at : at + cin], b, c)
        outs.append(total)
    out_ref[...] = jnp.swapaxes(jnp.stack(outs), 0, 1).astype(jnp.bfloat16)


def split_planes(feats, grads):
    planes, width = feats.shape[1:]
    rows = feats.shape[0] + grads.shape[0]
    one = jax.ShapeDtypeStruct((rows, width), feats.dtype)
    mid = jax.ShapeDtypeStruct((planes - 2, rows, width), feats.dtype)
    return on_core(split_body, (one, mid, one), held=False)(feats, grads)


def own_terms(cin, head, mid, tail):
    rows, width = head.shape
    planes = mid.shape[0] + 2
    return on_core(
        functools.partial(own_body, cin),
        jax.ShapeDtypeStruct((ROWS * cin, 2 * (rows - cin)), jnp.float32),
        [pltpu.VMEM((planes * 9 * cin, width), jnp.bfloat16)],
    )(head, mid, tail)


def weight_tiles(cin, lo, head, tail, hi, own, factor):
    rows, width = lo.shape
    return on_core(
        functools.partial(edge_body, cin, factor),
        jax.ShapeDtypeStruct((ROWS // 8, cin // 2, 8, 2 * (rows - cin)), jnp.float32),
        [pltpu.VMEM((18 * cin, width), jnp.bfloat16), pltpu.VMEM(own.shape, jnp.float32)],
    )(lo, head, tail, hi, own)


def forward(cin, slabs, taps, bias):
    rows, width = slabs[0].shape
    planes = slabs[2].shape[0] + 2
    return on_core(
        functools.partial(forward_body, cin),
        jax.ShapeDtypeStruct((rows - cin, planes, width), jnp.bfloat16),
        [pltpu.VMEM(((planes + 2) * 9 * cin, width), jnp.bfloat16)],
        near=False,
    )(*slabs, taps, bias)


def backward(cin, slabs, taps, after):
    rows, width = slabs[0].shape
    planes = slabs[2].shape[0] + 2
    return on_core(
        functools.partial(backward_body, cin),
        jax.ShapeDtypeStruct((cin, planes, width), jnp.bfloat16),
        [pltpu.VMEM(((planes + 2) * (rows - cin), width), jnp.bfloat16)],
        near=False,
    )(*slabs, taps, after)


def swap(blocks, axes):
    return lax.all_to_all(blocks, axes, 0, 0, tiled=True)


def on_device(features_in, kernel_taps, channel_bias, upstream):
    feats, grads = features_in[0], upstream[0]
    cin, depth, width = feats.shape
    cout = grads.shape[0]
    cells_all = lax.axis_size(DP) * depth * lax.axis_size("gz") * width
    factor = 1.0 / math.sqrt(cells_all)
    head, mid, tail = split_planes(feats, grads)
    slabs = lax.axis_size("gz")
    lo = lax.ppermute(tail, "gz", [(i, i + 1) for i in range(slabs - 1)])
    hi = lax.ppermute(head, "gz", [(i + 1, i) for i in range(slabs - 1)])
    planes = (lo, head, mid, tail, hi)
    kernel = kernel_taps.reshape(27, cin, cout)
    ahead = kernel.reshape(27 * cin, cout).T
    back = kernel[::-1].reshape(3, 9, cin, cout).transpose(1, 2, 0, 3).reshape(9 * cin, 3 * cout)
    own = own_terms(cin, head, mid, tail)
    tiles = weight_tiles(cin, lo, head, tail, hi, own, factor).reshape(TILES, 8, 128)
    part = jnp.sum(swap(tiles, NEAR), axis=0)
    output = forward(cin, planes, ahead, channel_bias[:, None])
    part, output = lax.optimization_barrier((part, output))
    grad_input = backward(cin, planes, back, part)
    far = lax.axis_size("dp_0")
    part = jnp.sum(swap(jnp.broadcast_to(part, (far, *part.shape)), "dp_0"), axis=0)
    part, grad_input = lax.optimization_barrier((part, grad_input))
    total = swap(jnp.broadcast_to(part.astype(jnp.bfloat16), tiles.shape), NEAR).astype(jnp.float32)
    total = total.reshape(4, 16, 8, 128).transpose(0, 2, 1, 3).reshape(ROWS, 2048)
    return (output[None], grad_input[None], total[:27], total[27, :cout])


def solution(mesh):
    split = Mesh(mesh.devices.reshape(16, 8, 2, mesh.shape["gz"]), ("dp_0", "dp_1", "dp_2", "gz"))
    placed = (P(DP, None, "gz", None), P(), P(), P(DP, None, "gz", None))
    return jax.shard_map(
        on_device,
        mesh=split,
        in_specs=placed,
        out_specs=(P(DP, None, "gz", None), P(DP, None, "gz", None), P(), P()),
        check_vma=False,
    )
```

```python
import functools
import math

import jax
import jax.numpy as jnp
from jax import lax
from jax.experimental import pallas as pl
from jax.experimental.pallas import tpu as pltpu
from jax.sharding import Mesh
from jax.sharding import PartitionSpec as P

NX = 64
NY = 8
DP = ("dp_0", "dp_1", "dp_2")
NEAR = ("dp_1", "dp_2", "gz")
TILES = 64
ROWS = 32
BIAS_ROW = 27
INTERPRET = False
VMEM = pl.BlockSpec(memory_space=pltpu.VMEM)


def on_core(body, out_shape, scratch=(), held=True, near=True):
    def call(*operands):
        if held:
            operands = [pltpu.with_memory_space_constraint(x, pltpu.VMEM) for x in operands]
        return pl.pallas_call(
            body,
            out_shape=jax.tree.map(lambda s: pltpu.VMEM(s.shape, s.dtype), out_shape) if near else out_shape,
            in_specs=[VMEM] * len(operands),
            out_specs=jax.tree.map(lambda _: VMEM, out_shape),
            scratch_shapes=list(scratch),
            interpret=INTERPRET,
        )(*operands)

    return call


def inside(width, db, dc):
    lane = lax.broadcasted_iota(jnp.int32, (1, width), 1)
    x = (lane & (NX - 1)) + dc
    y = lax.shift_right_logical(lane, NX.bit_length() - 1) + db
    return (x >= 0) & (x < NX) & (y >= 0) & (y < NY)


def moved(plane, b, c):
    width = plane.shape[-1]
    off = (b - 1) * NX + c - 1
    if off == 0:
        return plane
    return jnp.where(inside(width, b - 1, c - 1), pltpu.roll(plane, (-off) % width, 1), 0.0)


def store_moved(s_ref, at, plane):
    plane = plane.astype(jnp.float32)
    chans = plane.shape[0]
    for b in range(3):
        for c in range(3):
            row = at + (3 * b + c) * chans
            s_ref[row : row + chans, :] = moved(plane, b, c).astype(jnp.bfloat16)


def split_body(f_ref, u_ref, head_ref, mid_ref, tail_ref):
    cin, planes, _ = f_ref.shape
    for ref, at in ((f_ref, 0), (u_ref, cin)):
        rows = slice(at, at + ref.shape[0])
        own = jnp.swapaxes(ref[...].astype(jnp.float32), 0, 1).astype(jnp.bfloat16)
        head_ref[rows, :] = own[0]
        tail_ref[rows, :] = own[planes - 1]
        for z in range(1, planes - 1):
            mid_ref[z - 1, rows, :] = own[z]


def planes_of(head_ref, mid_ref, tail_ref, rows):
    mid = [mid_ref[z, rows, :] for z in range(mid_ref.shape[0])]
    return [head_ref[rows, :], *mid, tail_ref[rows, :]]


NT = (((1,), (1,)), ((), ()))


def dot(a, b, dims=(((1,), (0,)), ((), ()))):
    return lax.dot_general(a, b, dims, preferred_element_type=jnp.float32)


def own_body(cin, head_ref, mid_ref, tail_ref, w_ref, moved_ref, s_ref):
    width = head_ref.shape[1]
    cout = head_ref.shape[0] - cin
    taps = 9 * cin
    own = planes_of(head_ref, mid_ref, tail_ref, slice(0, cin))
    ups = planes_of(head_ref, mid_ref, tail_ref, slice(cin, cin + cout))
    planes = len(own)
    for z in range(planes):
        store_moved(s_ref, z * taps, own[z])
    moved_ref[...] = s_ref[:taps, :]
    twice = [jnp.concatenate([up, up], axis=0) for up in ups]
    for a in range(3):
        total = jnp.zeros((taps, 2 * cout), jnp.float32)
        for z in range(planes):
            src = z + a - 1
            if 0 <= src < planes:
                total += dot(s_ref[src * taps : (src + 1) * taps, :], twice[z], NT)
        w_ref[a * taps : (a + 1) * taps, :] = total
    ones = jnp.ones((16, width), jnp.bfloat16)
    bias = jnp.zeros((16, 2 * cout), jnp.float32)
    for z in range(planes):
        bias += dot(ones, twice[z], NT)
    w_ref[3 * taps :, :] = jnp.zeros((w_ref.shape[0] - 3 * taps, 2 * cout), jnp.float32)
    for row in (BIAS_ROW, BIAS_ROW + 1):
        w_ref[row * cin : row * cin + 8, :] = bias[:8]


def edge_body(cin, factor, lo_ref, head_ref, moved_ref, w_ref, tiles_ref, s_ref, v_ref):
    cout = lo_ref.shape[0] - cin
    taps = 9 * cin
    v_ref[...] = w_ref[...]
    store_moved(s_ref, 0, lo_ref[:cin, :])
    for a, sources_ref, up in ((0, s_ref, head_ref[cin:, :]), (2, moved_ref, lo_ref[cin:, :])):
        twice = jnp.concatenate([up, up], axis=0)
        v_ref[a * taps : (a + 1) * taps, :] += dot(sources_ref[...], twice, NT)
    left = lax.broadcasted_iota(jnp.int32, (ROWS, 2 * cout), 1) < cout
    for at in range(cin // 2):
        even = v_ref[pl.ds(2 * at, ROWS, stride=cin), :]
        odd = v_ref[pl.ds(2 * at + 1, ROWS, stride=cin), :]
        tiles_ref[:, at] = (jnp.where(left, even, odd) * factor).reshape(ROWS // 8, 8, 2 * cout)


def forward_body(cin, lo_ref, head_ref, mid_ref, tail_ref, hi_ref, w_ref, bias_ref, out_ref, s_ref):
    taps = 9 * cin
    rows = slice(0, cin)
    slabs = [lo_ref[rows, :], *planes_of(head_ref, mid_ref, tail_ref, rows), hi_ref[rows, :]]
    for z, plane in enumerate(slabs):
        store_moved(s_ref, z * taps, plane)
    outs = [dot(w_ref[...], s_ref[z * taps : (z + 3) * taps, :]) + bias_ref[...] for z in range(len(slabs) - 2)]
    out_ref[...] = jnp.swapaxes(jnp.stack(outs), 0, 1).astype(jnp.bfloat16)


def backward_body(cin, lo_ref, head_ref, mid_ref, tail_ref, hi_ref, w_ref, _, out_ref, p_ref):
    width = lo_ref.shape[1]
    cout = lo_ref.shape[0] - cin
    rows = slice(cin, cin + cout)
    slabs = [lo_ref[rows, :], *planes_of(head_ref, mid_ref, tail_ref, rows), hi_ref[rows, :]]
    for z, plane in enumerate(slabs):
        p_ref[z * cout : (z + 1) * cout, :] = plane
    outs = []
    for z in range(len(slabs) - 2):
        parts = dot(w_ref[...], p_ref[z * cout : (z + 3) * cout, :])
        total = jnp.zeros((cin, width), jnp.float32)
        for b in range(3):
            for c in range(3):
                at = (3 * b + c) * cin
                total += moved(parts[at : at + cin], b, c)
        outs.append(total)
    out_ref[...] = jnp.swapaxes(jnp.stack(outs), 0, 1).astype(jnp.bfloat16)


def split_planes(feats, grads):
    planes, width = feats.shape[1:]
    rows = feats.shape[0] + grads.shape[0]
    one = jax.ShapeDtypeStruct((rows, width), feats.dtype)
    mid = jax.ShapeDtypeStruct((planes - 2, rows, width), feats.dtype)
    return on_core(split_body, (one, mid, one), held=False)(feats, grads)


def own_terms(cin, head, mid, tail):
    rows, width = head.shape
    planes = mid.shape[0] + 2
    return on_core(
        functools.partial(own_body, cin),
        (jax.ShapeDtypeStruct((ROWS * cin, 2 * (rows - cin)), jnp.float32), jax.ShapeDtypeStruct((9 * cin, width), jnp.bfloat16)),
        [pltpu.VMEM((planes * 9 * cin, width), jnp.bfloat16)],
    )(head, mid, tail)


def weight_tiles(cin, lo, head, head_moved, own, factor):
    rows, width = lo.shape
    return on_core(
        functools.partial(edge_body, cin, factor),
        jax.ShapeDtypeStruct((ROWS // 8, cin // 2, 8, 2 * (rows - cin)), jnp.float32),
        [pltpu.VMEM((9 * cin, width), jnp.bfloat16), pltpu.VMEM(own.shape, jnp.float32)],
    )(lo, head, head_moved, own)


def forward(cin, slabs, taps, bias):
    rows, width = slabs[0].shape
    planes = slabs[2].shape[0] + 2
    return on_core(
        functools.partial(forward_body, cin),
        jax.ShapeDtypeStruct((rows - cin, planes, width), jnp.bfloat16),
        [pltpu.VMEM(((planes + 2) * 9 * cin, width), jnp.bfloat16)],
        near=False,
    )(*slabs, taps, bias)


def backward(cin, slabs, taps, after):
    rows, width = slabs[0].shape
    planes = slabs[2].shape[0] + 2
    return on_core(
        functools.partial(backward_body, cin),
        jax.ShapeDtypeStruct((cin, planes, width), jnp.bfloat16),
        [pltpu.VMEM(((planes + 2) * (rows - cin), width), jnp.bfloat16)],
        near=False,
    )(*slabs, taps, after)


def swap(blocks, axes):
    return lax.all_to_all(blocks, axes, 0, 0, tiled=True)


def on_device(features_in, kernel_taps, channel_bias, upstream):
    feats, grads = features_in[0], upstream[0]
    cin, depth, width = feats.shape
    cout = grads.shape[0]
    cells_all = lax.axis_size(DP) * depth * lax.axis_size("gz") * width
    factor = 1.0 / math.sqrt(cells_all)
    head, mid, tail = split_planes(feats, grads)
    slabs = lax.axis_size("gz")
    with jax.named_scope("below"):
        lo = lax.ppermute(tail, "gz", [(i, i + 1) for i in range(slabs - 1)])
    own, head_moved = own_terms(cin, head, mid, tail)
    tiles = weight_tiles(cin, lo, head, head_moved, own, factor).reshape(TILES, 8, 128)
    tiles, head_late = lax.optimization_barrier((tiles, head))
    with jax.named_scope("gather_parts"):
        parts = swap(tiles, NEAR)
    with jax.named_scope("above"):
        hi = lax.ppermute(head_late, "gz", [(i + 1, i) for i in range(slabs - 1)])
    planes = (lo, head, mid, tail, hi)
    kernel = kernel_taps.reshape(27, cin, cout)
    ahead = kernel.reshape(27 * cin, cout).T
    back = kernel[::-1].reshape(3, 9, cin, cout).transpose(1, 2, 0, 3).reshape(9 * cin, 3 * cout)
    output = forward(cin, planes, ahead, channel_bias[:, None])
    part, output = lax.optimization_barrier((jnp.sum(parts, axis=0), output))
    grad_input = backward(cin, planes, back, part)
    far = lax.axis_size("dp_0")
    part = jnp.sum(swap(jnp.broadcast_to(part, (far, *part.shape)), "dp_0"), axis=0)
    part, grad_input = lax.optimization_barrier((part, grad_input))
    rounded = lax.reduce_precision(part, 8, 7)
    last = lax.axis_index(NEAR) >= TILES - TILES * 8 // ROWS
    rest = last & (lax.broadcasted_iota(jnp.int32, part.shape, 0) == (BIAS_ROW + 1) % 8)
    part = jnp.where(rest, part - rounded, rounded).astype(jnp.bfloat16)
    total = swap(jnp.broadcast_to(part, tiles.shape), NEAR).astype(jnp.float32)
    total = total.reshape(4, 16, 8, 128).transpose(0, 2, 1, 3).reshape(ROWS, 2048)
    bias_total = total[BIAS_ROW, :cout] + total[BIAS_ROW + 1, :cout]
    return (output[None], grad_input[None], total[:27], bias_total)


def solution(mesh):
    split = Mesh(mesh.devices.reshape(16, 8, 2, mesh.shape["gz"]), ("dp_0", "dp_1", "dp_2", "gz"))
    placed = (P(DP, None, "gz", None), P(), P(), P(DP, None, "gz", None))
    return jax.shard_map(
        on_device,
        mesh=split,
        in_specs=placed,
        out_specs=(P(DP, None, "gz", None), P(DP, None, "gz", None), P(), P()),
        check_vma=False,
    )
```

```python
import functools
import math

import jax
import jax.numpy as jnp
from jax import lax
from jax.experimental import pallas as pl
from jax.experimental.pallas import tpu as pltpu
from jax.sharding import Mesh
from jax.sharding import PartitionSpec as P

NX = 64
NY = 8
DP = ("dp_0", "dp_1", "dp_2")
CORE = "dp_2"
NEAR = ("dp_1", "gz")
TILES = 32
ROWS = 32
BIAS_ROW = 27
INTERPRET = False
VMEM = pl.BlockSpec(memory_space=pltpu.VMEM)
SMEM = pl.BlockSpec(memory_space=pltpu.SMEM)


def on_core(body, out_shape, scratch=(), held=True, near=True):
    def call(*operands):
        if held:
            operands = [x if x.ndim == 1 else pltpu.with_memory_space_constraint(x, pltpu.VMEM) for x in operands]
        return pl.pallas_call(
            body,
            out_shape=jax.tree.map(lambda s: pltpu.VMEM(s.shape, s.dtype), out_shape) if near else out_shape,
            in_specs=[SMEM if x.ndim == 1 else VMEM for x in operands],
            out_specs=jax.tree.map(lambda _: VMEM, out_shape),
            scratch_shapes=list(scratch),
            interpret=INTERPRET,
        )(*operands)

    return call


def inside(width, db, dc):
    lane = lax.broadcasted_iota(jnp.int32, (1, width), 1)
    x = (lane & (NX - 1)) + dc
    y = lax.shift_right_logical(lane, NX.bit_length() - 1) + db
    return (x >= 0) & (x < NX) & (y >= 0) & (y < NY)


def moved(plane, b, c):
    width = plane.shape[-1]
    off = (b - 1) * NX + c - 1
    if off == 0:
        return plane
    return jnp.where(inside(width, b - 1, c - 1), pltpu.roll(plane, (-off) % width, 1), 0.0)


def store_moved(s_ref, at, plane):
    plane = plane.astype(jnp.float32)
    chans = plane.shape[0]
    for b in range(3):
        for c in range(3):
            row = at + (3 * b + c) * chans
            s_ref[row : row + chans, :] = moved(plane, b, c).astype(jnp.bfloat16)


def split_body(f_ref, u_ref, head_ref, mid_ref, tail_ref):
    cin, planes, _ = f_ref.shape
    for ref, at in ((f_ref, 0), (u_ref, cin)):
        rows = slice(at, at + ref.shape[0])
        own = jnp.swapaxes(ref[...].astype(jnp.float32), 0, 1).astype(jnp.bfloat16)
        head_ref[rows, :] = own[0]
        tail_ref[rows, :] = own[planes - 1]
        for z in range(1, planes - 1):
            mid_ref[z - 1, rows, :] = own[z]


def planes_of(head_ref, mid_ref, tail_ref, rows):
    mid = [mid_ref[z, rows, :] for z in range(mid_ref.shape[0])]
    return [head_ref[rows, :], *mid, tail_ref[rows, :]]


NT = (((1,), (1,)), ((), ()))


def dot(a, b, dims=(((1,), (0,)), ((), ()))):
    return lax.dot_general(a, b, dims, preferred_element_type=jnp.float32)


def own_body(cin, head_ref, mid_ref, tail_ref, w_ref, moved_ref, s_ref):
    width = head_ref.shape[1]
    cout = head_ref.shape[0] - cin
    taps = 9 * cin
    own = planes_of(head_ref, mid_ref, tail_ref, slice(0, cin))
    ups = planes_of(head_ref, mid_ref, tail_ref, slice(cin, cin + cout))
    planes = len(own)
    for z in range(planes):
        store_moved(s_ref, z * taps, own[z])
    moved_ref[...] = s_ref[:taps, :]
    twice = [jnp.concatenate([up, up], axis=0) for up in ups]
    for a in range(3):
        total = jnp.zeros((taps, 2 * cout), jnp.float32)
        for z in range(planes):
            src = z + a - 1
            if 0 <= src < planes:
                total += dot(s_ref[src * taps : (src + 1) * taps, :], twice[z], NT)
        w_ref[a * taps : (a + 1) * taps, :] = total
    ones = jnp.ones((16, width), jnp.bfloat16)
    bias = jnp.zeros((16, 2 * cout), jnp.float32)
    for z in range(planes):
        bias += dot(ones, twice[z], NT)
    w_ref[3 * taps :, :] = jnp.zeros((w_ref.shape[0] - 3 * taps, 2 * cout), jnp.float32)
    for row in (BIAS_ROW, BIAS_ROW + 1):
        w_ref[row * cin : row * cin + 8, :] = bias[:8]


def edge_body(cin, factor, core_ref, lo_ref, head_ref, moved_ref, w_ref, keep_ref, send_ref, s_ref, v_ref):
    cout = lo_ref.shape[0] - cin
    taps = 9 * cin
    v_ref[...] = w_ref[...]
    store_moved(s_ref, 0, lo_ref[:cin, :])
    for a, sources_ref, up in ((0, s_ref, head_ref[cin:, :]), (2, moved_ref, lo_ref[cin:, :])):
        twice = jnp.concatenate([up, up], axis=0)
        v_ref[a * taps : (a + 1) * taps, :] += dot(sources_ref[...], twice, NT)
    left = lax.broadcasted_iota(jnp.int32, (ROWS, 2 * cout), 1) < cout
    first = core_ref[0] == 0
    for at in range(cin // 2):
        even = v_ref[pl.ds(2 * at, ROWS, stride=cin), :]
        odd = v_ref[pl.ds(2 * at + 1, ROWS, stride=cin), :]
        both = (jnp.where(left, even, odd) * factor).reshape(2, ROWS // 16, 8, 2 * cout)
        keep_ref[:, at] = jnp.where(first, both[0], both[1])
        send_ref[:, at] = jnp.where(first, both[1], both[0])


def forward_body(cin, lo_ref, head_ref, mid_ref, tail_ref, hi_ref, w_ref, bias_ref, _, out_ref, s_ref):
    taps = 9 * cin
    rows = slice(0, cin)
    slabs = [lo_ref[rows, :], *planes_of(head_ref, mid_ref, tail_ref, rows), hi_ref[rows, :]]
    for z, plane in enumerate(slabs):
        store_moved(s_ref, z * taps, plane)
    outs = [dot(w_ref[...], s_ref[z * taps : (z + 3) * taps, :]) + bias_ref[...] for z in range(len(slabs) - 2)]
    out_ref[...] = jnp.swapaxes(jnp.stack(outs), 0, 1).astype(jnp.bfloat16)


def backward_body(cin, lo_ref, head_ref, mid_ref, tail_ref, hi_ref, w_ref, _, out_ref, p_ref):
    width = lo_ref.shape[1]
    cout = lo_ref.shape[0] - cin
    rows = slice(cin, cin + cout)
    slabs = [lo_ref[rows, :], *planes_of(head_ref, mid_ref, tail_ref, rows), hi_ref[rows, :]]
    for z, plane in enumerate(slabs):
        p_ref[z * cout : (z + 1) * cout, :] = plane
    outs = []
    for z in range(len(slabs) - 2):
        parts = dot(w_ref[...], p_ref[z * cout : (z + 3) * cout, :])
        total = jnp.zeros((cin, width), jnp.float32)
        for b in range(3):
            for c in range(3):
                at = (3 * b + c) * cin
                total += moved(parts[at : at + cin], b, c)
        outs.append(total)
    out_ref[...] = jnp.swapaxes(jnp.stack(outs), 0, 1).astype(jnp.bfloat16)


def split_planes(feats, grads):
    planes, width = feats.shape[1:]
    rows = feats.shape[0] + grads.shape[0]
    one = jax.ShapeDtypeStruct((rows, width), feats.dtype)
    mid = jax.ShapeDtypeStruct((planes - 2, rows, width), feats.dtype)
    return on_core(split_body, (one, mid, one), held=False)(feats, grads)


def own_terms(cin, head, mid, tail):
    rows, width = head.shape
    planes = mid.shape[0] + 2
    return on_core(
        functools.partial(own_body, cin),
        (jax.ShapeDtypeStruct((ROWS * cin, 2 * (rows - cin)), jnp.float32), jax.ShapeDtypeStruct((9 * cin, width), jnp.bfloat16)),
        [pltpu.VMEM((planes * 9 * cin, width), jnp.bfloat16)],
    )(head, mid, tail)


def weight_tiles(cin, core, lo, head, head_moved, own, factor):
    rows, width = lo.shape
    half = jax.ShapeDtypeStruct((ROWS // 16, cin // 2, 8, 2 * (rows - cin)), jnp.float32)
    return on_core(
        functools.partial(edge_body, cin, factor),
        (half, half),
        [pltpu.VMEM((9 * cin, width), jnp.bfloat16), pltpu.VMEM(own.shape, jnp.float32)],
    )(core, lo, head, head_moved, own)


def forward(cin, slabs, taps, bias, after):
    rows, width = slabs[0].shape
    planes = slabs[2].shape[0] + 2
    return on_core(
        functools.partial(forward_body, cin),
        jax.ShapeDtypeStruct((rows - cin, planes, width), jnp.bfloat16),
        [pltpu.VMEM(((planes + 2) * 9 * cin, width), jnp.bfloat16)],
        near=False,
    )(*slabs, taps, bias, after)


def backward(cin, slabs, taps, after):
    rows, width = slabs[0].shape
    planes = slabs[2].shape[0] + 2
    return on_core(
        functools.partial(backward_body, cin),
        jax.ShapeDtypeStruct((cin, planes, width), jnp.bfloat16),
        [pltpu.VMEM(((planes + 2) * (rows - cin), width), jnp.bfloat16)],
        near=False,
    )(*slabs, taps, after)


def swap(blocks, axes):
    return lax.all_to_all(blocks, axes, 0, 0, tiled=True)


def on_device(features_in, kernel_taps, channel_bias, upstream):
    feats, grads = features_in[0], upstream[0]
    cin, depth, width = feats.shape
    cout = grads.shape[0]
    cells_all = lax.axis_size(DP) * depth * lax.axis_size("gz") * width
    factor = 1.0 / math.sqrt(cells_all)
    head, mid, tail = split_planes(feats, grads)
    slabs = lax.axis_size("gz")
    with jax.named_scope("below"):
        lo = lax.ppermute(tail, "gz", [(i, i + 1) for i in range(slabs - 1)])
    own, head_moved = own_terms(cin, head, mid, tail)
    core = lax.axis_index(CORE)
    keep, send = weight_tiles(cin, core[None], lo, head, head_moved, own, factor)
    tiles = (keep + lax.ppermute(send, CORE, [(0, 1), (1, 0)])).reshape(TILES, 8, 128)
    tiles, head_late = lax.optimization_barrier((tiles, head))
    parts = swap(tiles, NEAR)
    hi = lax.ppermute(head_late, "gz", [(i + 1, i) for i in range(slabs - 1)])
    kernel = kernel_taps.reshape(27, cin, cout)
    ahead = kernel.reshape(27 * cin, cout).T
    back = kernel[::-1].reshape(3, 9, cin, cout).transpose(1, 2, 0, 3).reshape(9 * cin, 3 * cout)
    bias = channel_bias[:, None]
    part, hi, ahead, back, bias = lax.optimization_barrier((jnp.sum(parts, axis=0), hi, ahead, back, bias))
    planes = (lo, head, mid, tail, hi)
    output = forward(cin, planes, ahead, bias, part)
    grad_input = backward(cin, planes, back, part)
    far = lax.axis_size("dp_0")
    part = jnp.sum(swap(jnp.broadcast_to(part, (far, *part.shape)), "dp_0"), axis=0)
    part, output, grad_input = lax.optimization_barrier((part, output, grad_input))
    rounded = lax.reduce_precision(part, 8, 7)
    last = core * TILES + lax.axis_index(NEAR) >= BIAS_ROW // 8 * (cin // 2)
    rest = last & (lax.broadcasted_iota(jnp.int32, part.shape, 0) == (BIAS_ROW + 1) % 8)
    part = jnp.where(rest, part - rounded, rounded).astype(jnp.bfloat16)
    total = lax.all_gather(swap(jnp.broadcast_to(part, tiles.shape), NEAR), CORE).astype(jnp.float32)
    total = total.reshape(4, 16, 8, 128).transpose(0, 2, 1, 3).reshape(ROWS, 2048)
    bias_total = total[BIAS_ROW, :cout] + total[BIAS_ROW + 1, :cout]
    return (output[None], grad_input[None], total[:27], bias_total)


def solution(mesh):
    split = Mesh(mesh.devices.reshape(16, 8, 2, mesh.shape["gz"]), ("dp_0", "dp_1", "dp_2", "gz"))
    placed = (P(DP, None, "gz", None), P(), P(), P(DP, None, "gz", None))
    return jax.shard_map(
        on_device,
        mesh=split,
        in_specs=placed,
        out_specs=(P(DP, None, "gz", None), P(DP, None, "gz", None), P(), P()),
        check_vma=False,
    )
```

```python
import functools
import math

import jax
import jax.numpy as jnp
from jax import lax
from jax.experimental import pallas as pl
from jax.experimental.pallas import tpu as pltpu
from jax.sharding import Mesh
from jax.sharding import PartitionSpec as P

NX = 64
NY = 8
DP = ("dp_0", "dp_1", "dp_2")
CORE = "dp_2"
NEAR = ("dp_1", "gz")
TILES = 32
ROWS = 32
BIAS_ROW = 27
INTERPRET = False
VMEM = pl.BlockSpec(memory_space=pltpu.VMEM)
SMEM = pl.BlockSpec(memory_space=pltpu.SMEM)


def on_core(body, out_shape, scratch=(), held=True, near=True):
    def call(*operands):
        if held:
            operands = [x if x.ndim == 1 else pltpu.with_memory_space_constraint(x, pltpu.VMEM) for x in operands]
        return pl.pallas_call(
            body,
            out_shape=jax.tree.map(lambda s: pltpu.VMEM(s.shape, s.dtype), out_shape) if near else out_shape,
            in_specs=[SMEM if x.ndim == 1 else VMEM for x in operands],
            out_specs=jax.tree.map(lambda _: VMEM, out_shape),
            scratch_shapes=list(scratch),
            interpret=INTERPRET,
        )(*operands)

    return call


def inside(width, db, dc):
    lane = lax.broadcasted_iota(jnp.int32, (1, width), 1)
    x = (lane & (NX - 1)) + dc
    y = lax.shift_right_logical(lane, NX.bit_length() - 1) + db
    return (x >= 0) & (x < NX) & (y >= 0) & (y < NY)


def moved(plane, b, c):
    width = plane.shape[-1]
    off = (b - 1) * NX + c - 1
    if off == 0:
        return plane
    return jnp.where(inside(width, b - 1, c - 1), pltpu.roll(plane, (-off) % width, 1), 0.0)


def store_moved(s_ref, at, plane):
    plane = plane.astype(jnp.float32)
    chans = plane.shape[0]
    for b in range(3):
        for c in range(3):
            row = at + (3 * b + c) * chans
            s_ref[row : row + chans, :] = moved(plane, b, c).astype(jnp.bfloat16)


def split_body(f_ref, u_ref, head_ref, mid_ref, tail_ref):
    cin, planes, _ = f_ref.shape
    for ref, at in ((f_ref, 0), (u_ref, cin)):
        rows = slice(at, at + ref.shape[0])
        own = jnp.swapaxes(ref[...].astype(jnp.float32), 0, 1).astype(jnp.bfloat16)
        head_ref[rows, :] = own[0]
        tail_ref[rows, :] = own[planes - 1]
        for z in range(1, planes - 1):
            mid_ref[z - 1, rows, :] = own[z]


def planes_of(head_ref, mid_ref, tail_ref, rows):
    mid = [mid_ref[z, rows, :] for z in range(mid_ref.shape[0])]
    return [head_ref[rows, :], *mid, tail_ref[rows, :]]


NT = (((1,), (1,)), ((), ()))


def dot(a, b, dims=(((1,), (0,)), ((), ()))):
    return lax.dot_general(a, b, dims, preferred_element_type=jnp.float32)


def own_body(cin, head_ref, mid_ref, tail_ref, w_ref, moved_ref, s_ref):
    width = head_ref.shape[1]
    cout = head_ref.shape[0] - cin
    taps = 9 * cin
    own = planes_of(head_ref, mid_ref, tail_ref, slice(0, cin))
    ups = planes_of(head_ref, mid_ref, tail_ref, slice(cin, cin + cout))
    planes = len(own)
    for z in range(planes):
        store_moved(s_ref, z * taps, own[z])
    moved_ref[...] = s_ref[:taps, :]
    twice = [jnp.concatenate([up, up], axis=0) for up in ups]
    for a in range(3):
        total = jnp.zeros((taps, 2 * cout), jnp.float32)
        for z in range(planes):
            src = z + a - 1
            if 0 <= src < planes:
                total += dot(s_ref[src * taps : (src + 1) * taps, :], twice[z], NT)
        w_ref[a * taps : (a + 1) * taps, :] = total
    ones = jnp.ones((16, width), jnp.bfloat16)
    bias = jnp.zeros((16, 2 * cout), jnp.float32)
    for z in range(planes):
        bias += dot(ones, twice[z], NT)
    w_ref[3 * taps :, :] = jnp.zeros((w_ref.shape[0] - 3 * taps, 2 * cout), jnp.float32)
    for row in (BIAS_ROW, BIAS_ROW + 1):
        w_ref[row * cin : row * cin + 8, :] = bias[:8]


def edge_body(cin, factor, core_ref, lo_ref, head_ref, moved_ref, w_ref, keep_ref, send_ref, s_ref, v_ref):
    cout = lo_ref.shape[0] - cin
    taps = 9 * cin
    v_ref[...] = w_ref[...]
    store_moved(s_ref, 0, lo_ref[:cin, :])
    for a, sources_ref, up in ((0, s_ref, head_ref[cin:, :]), (2, moved_ref, lo_ref[cin:, :])):
        twice = jnp.concatenate([up, up], axis=0)
        v_ref[a * taps : (a + 1) * taps, :] += dot(sources_ref[...], twice, NT)
    left = lax.broadcasted_iota(jnp.int32, (ROWS, 2 * cout), 1) < cout
    first = core_ref[0] == 0
    for at in range(cin // 2):
        even = v_ref[pl.ds(2 * at, ROWS, stride=cin), :]
        odd = v_ref[pl.ds(2 * at + 1, ROWS, stride=cin), :]
        both = (jnp.where(left, even, odd) * factor).reshape(2, ROWS // 16, 8, 2 * cout)
        keep_ref[:, at] = jnp.where(first, both[0], both[1])
        send_ref[:, at] = jnp.where(first, both[1], both[0])


def forward_body(cin, lo_ref, head_ref, mid_ref, tail_ref, hi_ref, w_ref, bias_ref, _, out_ref, s_ref):
    taps = 9 * cin
    rows = slice(0, cin)
    slabs = [lo_ref[rows, :], *planes_of(head_ref, mid_ref, tail_ref, rows), hi_ref[rows, :]]
    for z, plane in enumerate(slabs):
        store_moved(s_ref, z * taps, plane)
    outs = [dot(w_ref[...], s_ref[z * taps : (z + 3) * taps, :]) + bias_ref[...] for z in range(len(slabs) - 2)]
    out_ref[...] = jnp.swapaxes(jnp.stack(outs), 0, 1).astype(jnp.bfloat16)


def backward_body(cin, lo_ref, head_ref, mid_ref, tail_ref, hi_ref, w_ref, _, out_ref, p_ref):
    width = lo_ref.shape[1]
    cout = lo_ref.shape[0] - cin
    rows = slice(cin, cin + cout)
    slabs = [lo_ref[rows, :], *planes_of(head_ref, mid_ref, tail_ref, rows), hi_ref[rows, :]]
    for z, plane in enumerate(slabs):
        p_ref[z * cout : (z + 1) * cout, :] = plane
    outs = []
    for z in range(len(slabs) - 2):
        parts = dot(w_ref[...], p_ref[z * cout : (z + 3) * cout, :])
        total = jnp.zeros((cin, width), jnp.float32)
        for b in range(3):
            for c in range(3):
                at = (3 * b + c) * cin
                total += moved(parts[at : at + cin], b, c)
        outs.append(total)
    out_ref[...] = jnp.swapaxes(jnp.stack(outs), 0, 1).astype(jnp.bfloat16)


def split_planes(feats, grads):
    planes, width = feats.shape[1:]
    rows = feats.shape[0] + grads.shape[0]
    one = jax.ShapeDtypeStruct((rows, width), feats.dtype)
    mid = jax.ShapeDtypeStruct((planes - 2, rows, width), feats.dtype)
    return on_core(split_body, (one, mid, one), held=False)(feats, grads)


def own_terms(cin, head, mid, tail):
    rows, width = head.shape
    planes = mid.shape[0] + 2
    return on_core(
        functools.partial(own_body, cin),
        (jax.ShapeDtypeStruct((ROWS * cin, 2 * (rows - cin)), jnp.float32), jax.ShapeDtypeStruct((9 * cin, width), jnp.bfloat16)),
        [pltpu.VMEM((planes * 9 * cin, width), jnp.bfloat16)],
    )(head, mid, tail)


def weight_tiles(cin, core, lo, head, head_moved, own, factor):
    rows, width = lo.shape
    half = jax.ShapeDtypeStruct((ROWS // 16, cin // 2, 8, 2 * (rows - cin)), jnp.float32)
    return on_core(
        functools.partial(edge_body, cin, factor),
        (half, half),
        [pltpu.VMEM((9 * cin, width), jnp.bfloat16), pltpu.VMEM(own.shape, jnp.float32)],
    )(core, lo, head, head_moved, own)


def forward(cin, slabs, taps, bias, after):
    rows, width = slabs[0].shape
    planes = slabs[2].shape[0] + 2
    return on_core(
        functools.partial(forward_body, cin),
        jax.ShapeDtypeStruct((rows - cin, planes, width), jnp.bfloat16),
        [pltpu.VMEM(((planes + 2) * 9 * cin, width), jnp.bfloat16)],
        near=False,
    )(*slabs, taps, bias, after)


def backward(cin, slabs, taps, after):
    rows, width = slabs[0].shape
    planes = slabs[2].shape[0] + 2
    return on_core(
        functools.partial(backward_body, cin),
        jax.ShapeDtypeStruct((cin, planes, width), jnp.bfloat16),
        [pltpu.VMEM(((planes + 2) * (rows - cin), width), jnp.bfloat16)],
        near=False,
    )(*slabs, taps, after)


def swap(blocks, axes):
    return lax.all_to_all(blocks, axes, 0, 0, tiled=True)


def on_device(features_in, kernel_taps, channel_bias, upstream):
    feats, grads = features_in[0], upstream[0]
    cin, depth, width = feats.shape
    cout = grads.shape[0]
    cells_all = lax.axis_size(DP) * depth * lax.axis_size("gz") * width
    factor = 1.0 / math.sqrt(cells_all)
    head, mid, tail = split_planes(feats, grads)
    slabs = lax.axis_size("gz")
    with jax.named_scope("below"):
        lo = lax.ppermute(tail, "gz", [(i, i + 1) for i in range(slabs - 1)])
    own, head_moved = own_terms(cin, head, mid, tail)
    core = lax.axis_index(CORE)
    keep, send = weight_tiles(cin, core[None], lo, head, head_moved, own, factor)
    tiles = (keep + lax.ppermute(send, CORE, [(0, 1), (1, 0)])).reshape(TILES, 8, 128)
    tiles, head_late = lax.optimization_barrier((tiles, head))
    parts = swap(tiles, NEAR)
    hi = lax.ppermute(head_late, "gz", [(i + 1, i) for i in range(slabs - 1)])
    kernel = kernel_taps.reshape(27, cin, cout)
    ahead = kernel.reshape(27 * cin, cout).T
    back = kernel[::-1].reshape(3, 9, cin, cout).transpose(1, 2, 0, 3).reshape(9 * cin, 3 * cout)
    bias = channel_bias[:, None]
    part, ahead, back, bias = lax.optimization_barrier((jnp.sum(parts, axis=0), ahead, back, bias))
    planes = (lo, head, mid, tail, hi)
    output = forward(cin, planes, ahead, bias, part)
    grad_input = backward(cin, planes, back, part)
    far = lax.axis_size("dp_0")
    part = jnp.sum(swap(jnp.broadcast_to(part, (far, *part.shape)), "dp_0"), axis=0)
    part, output, grad_input = lax.optimization_barrier((part, output, grad_input))
    rounded = lax.reduce_precision(part, 8, 7)
    last = core * TILES + lax.axis_index(NEAR) >= BIAS_ROW // 8 * (cin // 2)
    rest = last & (lax.broadcasted_iota(jnp.int32, part.shape, 0) == (BIAS_ROW + 1) % 8)
    part = jnp.where(rest, part - rounded, rounded).astype(jnp.bfloat16)
    total = swap(jnp.broadcast_to(part, (2 * TILES, *part.shape)), (CORE, *NEAR)).astype(jnp.float32)
    total = total.reshape(4, 16, 8, 128).transpose(0, 2, 1, 3).reshape(ROWS, 2048)
    bias_total = total[BIAS_ROW, :cout] + total[BIAS_ROW + 1, :cout]
    return (output[None], grad_input[None], total[:27], bias_total)


def solution(mesh):
    split = Mesh(mesh.devices.reshape(16, 8, 2, mesh.shape["gz"]), ("dp_0", "dp_1", "dp_2", "gz"))
    placed = (P(DP, None, "gz", None), P(), P(), P(DP, None, "gz", None))
    return jax.shard_map(
        on_device,
        mesh=split,
        in_specs=placed,
        out_specs=(P(DP, None, "gz", None), P(DP, None, "gz", None), P(), P()),
        check_vma=False,
    )
```

```python
import functools
import math

import jax
import jax.numpy as jnp
from jax import lax
from jax.experimental import pallas as pl
from jax.experimental.pallas import tpu as pltpu
from jax.sharding import Mesh
from jax.sharding import PartitionSpec as P


NX = 64
NY = 8
DP = ("dp_0", "dp_1", "dp_2")
CORE = "dp_2"
NEAR = ("dp_1", "gz")
TILES = 32
ROWS = 32
BIAS_ROW = 27
INTERPRET = False
VMEM = pl.BlockSpec(memory_space=pltpu.VMEM)
SMEM = pl.BlockSpec(memory_space=pltpu.SMEM)


def on_core(body, out_shape, scratch=(), held=True, near=True):
    def call(*operands):
        if held:
            operands = [x if x.ndim == 1 else pltpu.with_memory_space_constraint(x, pltpu.VMEM) for x in operands]
        return pl.pallas_call(
            body,
            out_shape=jax.tree.map(lambda s: pltpu.VMEM(s.shape, s.dtype), out_shape) if near else out_shape,
            in_specs=[SMEM if x.ndim == 1 else VMEM for x in operands],
            out_specs=jax.tree.map(lambda _: VMEM, out_shape),
            scratch_shapes=list(scratch),
            interpret=INTERPRET,
        )(*operands)

    return call


def inside(width, db, dc):
    lane = lax.broadcasted_iota(jnp.int32, (1, width), 1)
    x = (lane & (NX - 1)) + dc
    y = lax.shift_right_logical(lane, NX.bit_length() - 1) + db
    return (x >= 0) & (x < NX) & (y >= 0) & (y < NY)


def moved(plane, b, c):
    width = plane.shape[-1]
    off = (b - 1) * NX + c - 1
    if off == 0:
        return plane
    return jnp.where(inside(width, b - 1, c - 1), pltpu.roll(plane, (-off) % width, 1), 0.0)


def store_moved(s_ref, at, plane):
    plane = plane.astype(jnp.float32)
    chans = plane.shape[0]
    for b in range(3):
        for c in range(3):
            row = at + (3 * b + c) * chans
            s_ref[row : row + chans, :] = moved(plane, b, c).astype(jnp.bfloat16)


def split_body(f_ref, u_ref, head_ref, mid_ref, tail_ref):
    cin, planes, _ = f_ref.shape
    for ref, at in ((f_ref, 0), (u_ref, cin)):
        rows = slice(at, at + ref.shape[0])
        own = jnp.swapaxes(ref[...].astype(jnp.float32), 0, 1).astype(jnp.bfloat16)
        head_ref[rows, :] = own[0]
        tail_ref[rows, :] = own[planes - 1]
        for z in range(1, planes - 1):
            mid_ref[z - 1, rows, :] = own[z]


def planes_of(head_ref, mid_ref, tail_ref, rows):
    mid = [mid_ref[z, rows, :] for z in range(mid_ref.shape[0])]
    return [head_ref[rows, :], *mid, tail_ref[rows, :]]


NT = (((1,), (1,)), ((), ()))


def dot(a, b, dims=(((1,), (0,)), ((), ()))):
    return lax.dot_general(a, b, dims, preferred_element_type=jnp.float32)


def own_body(cin, head_ref, mid_ref, tail_ref, w_ref, moved_ref, s_ref):
    width = head_ref.shape[1]
    cout = head_ref.shape[0] - cin
    taps = 9 * cin
    own = planes_of(head_ref, mid_ref, tail_ref, slice(0, cin))
    ups = planes_of(head_ref, mid_ref, tail_ref, slice(cin, cin + cout))
    planes = len(own)
    for z in range(planes):
        store_moved(s_ref, z * taps, own[z])
    moved_ref[...] = s_ref[:taps, :]
    twice = [jnp.concatenate([up, up], axis=0) for up in ups]
    for a in range(3):
        total = jnp.zeros((taps, 2 * cout), jnp.float32)
        for z in range(planes):
            src = z + a - 1
            if 0 <= src < planes:
                total += dot(s_ref[src * taps : (src + 1) * taps, :], twice[z], NT)
        w_ref[a * taps : (a + 1) * taps, :] = total
    ones = jnp.ones((16, width), jnp.bfloat16)
    bias = jnp.zeros((16, 2 * cout), jnp.float32)
    for z in range(planes):
        bias += dot(ones, twice[z], NT)
    w_ref[3 * taps :, :] = jnp.zeros((w_ref.shape[0] - 3 * taps, 2 * cout), jnp.float32)
    for row in (BIAS_ROW, BIAS_ROW + 1):
        w_ref[row * cin : row * cin + 8, :] = bias[:8]


def edge_body(cin, factor, core_ref, lo_ref, head_ref, moved_ref, w_ref, keep_ref, send_ref, s_ref, v_ref):
    cout = lo_ref.shape[0] - cin
    taps = 9 * cin
    v_ref[...] = w_ref[...]
    store_moved(s_ref, 0, lo_ref[:cin, :])
    for a, sources_ref, up in ((0, s_ref, head_ref[cin:, :]), (2, moved_ref, lo_ref[cin:, :])):
        twice = jnp.concatenate([up, up], axis=0)
        v_ref[a * taps : (a + 1) * taps, :] += dot(sources_ref[...], twice, NT)
    left = lax.broadcasted_iota(jnp.int32, (ROWS, 2 * cout), 1) < cout
    first = core_ref[0] == 0
    for at in range(cin // 2):
        even = v_ref[pl.ds(2 * at, ROWS, stride=cin), :]
        odd = v_ref[pl.ds(2 * at + 1, ROWS, stride=cin), :]
        both = (jnp.where(left, even, odd) * factor).reshape(2, ROWS // 16, 8, 2 * cout)
        keep_ref[:, at] = jnp.where(first, both[0], both[1])
        send_ref[:, at] = jnp.where(first, both[1], both[0])


def forward_body(cin, lo_ref, head_ref, mid_ref, tail_ref, hi_ref, w_ref, bias_ref, _, out_ref, s_ref):
    taps = 9 * cin
    rows = slice(0, cin)
    slabs = [lo_ref[rows, :], *planes_of(head_ref, mid_ref, tail_ref, rows), hi_ref[rows, :]]
    for z, plane in enumerate(slabs):
        store_moved(s_ref, z * taps, plane)
    outs = [dot(w_ref[...], s_ref[z * taps : (z + 3) * taps, :]) + bias_ref[...] for z in range(len(slabs) - 2)]
    out_ref[...] = jnp.swapaxes(jnp.stack(outs), 0, 1).astype(jnp.bfloat16)


def backward_body(cin, lo_ref, head_ref, mid_ref, tail_ref, hi_ref, w_ref, _, out_ref, p_ref):
    width = lo_ref.shape[1]
    cout = lo_ref.shape[0] - cin
    rows = slice(cin, cin + cout)
    slabs = [lo_ref[rows, :], *planes_of(head_ref, mid_ref, tail_ref, rows), hi_ref[rows, :]]
    for z, plane in enumerate(slabs):
        p_ref[z * cout : (z + 1) * cout, :] = plane
    outs = []
    for z in range(len(slabs) - 2):
        parts = dot(w_ref[...], p_ref[z * cout : (z + 3) * cout, :])
        total = jnp.zeros((cin, width), jnp.float32)
        for b in range(3):
            for c in range(3):
                at = (3 * b + c) * cin
                total += moved(parts[at : at + cin], b, c)
        outs.append(total)
    out_ref[...] = jnp.swapaxes(jnp.stack(outs), 0, 1).astype(jnp.bfloat16)


def split_planes(feats, grads):
    planes, width = feats.shape[1:]
    rows = feats.shape[0] + grads.shape[0]
    one = jax.ShapeDtypeStruct((rows, width), feats.dtype)
    mid = jax.ShapeDtypeStruct((planes - 2, rows, width), feats.dtype)
    return on_core(split_body, (one, mid, one), held=False)(feats, grads)


def own_terms(cin, head, mid, tail):
    rows, width = head.shape
    planes = mid.shape[0] + 2
    return on_core(
        functools.partial(own_body, cin),
        (jax.ShapeDtypeStruct((ROWS * cin, 2 * (rows - cin)), jnp.float32), jax.ShapeDtypeStruct((9 * cin, width), jnp.bfloat16)),
        [pltpu.VMEM((planes * 9 * cin, width), jnp.bfloat16)],
    )(head, mid, tail)


def weight_tiles(cin, core, lo, head, head_moved, own, factor):
    rows, width = lo.shape
    half = jax.ShapeDtypeStruct((ROWS // 16, cin // 2, 8, 2 * (rows - cin)), jnp.float32)
    return on_core(
        functools.partial(edge_body, cin, factor),
        (half, half),
        [pltpu.VMEM((9 * cin, width), jnp.bfloat16), pltpu.VMEM(own.shape, jnp.float32)],
    )(core, lo, head, head_moved, own)


def forward(cin, slabs, taps, bias, after):
    rows, width = slabs[0].shape
    planes = slabs[2].shape[0] + 2
    return on_core(
        functools.partial(forward_body, cin),
        jax.ShapeDtypeStruct((rows - cin, planes, width), jnp.bfloat16),
        [pltpu.VMEM(((planes + 2) * 9 * cin, width), jnp.bfloat16)],
        near=False,
    )(*slabs, taps, bias, after)


def backward(cin, slabs, taps, after):
    rows, width = slabs[0].shape
    planes = slabs[2].shape[0] + 2
    return on_core(
        functools.partial(backward_body, cin),
        jax.ShapeDtypeStruct((cin, planes, width), jnp.bfloat16),
        [pltpu.VMEM(((planes + 2) * (rows - cin), width), jnp.bfloat16)],
        near=False,
    )(*slabs, taps, after)


def swap(blocks, axes):
    return lax.all_to_all(blocks, axes, 0, 0, tiled=True)


def on_device(features_in, kernel_taps, channel_bias, upstream):
    feats, grads = features_in[0], upstream[0]
    cin, depth, width = feats.shape
    cout = grads.shape[0]
    cells_all = lax.axis_size(DP) * depth * lax.axis_size("gz") * width
    factor = 1.0 / math.sqrt(cells_all)
    head, mid, tail = split_planes(feats, grads)
    slabs = lax.axis_size("gz")
    lo = lax.ppermute(tail, "gz", [(i, i + 1) for i in range(slabs - 1)])
    own, head_moved = own_terms(cin, head, mid, tail)
    core = lax.axis_index(CORE)
    keep, send = weight_tiles(cin, core[None], lo, head, head_moved, own, factor)
    tiles = (keep + lax.ppermute(send, CORE, [(0, 1), (1, 0)])).reshape(TILES, 8, 128)
    tiles, head_late = lax.optimization_barrier((tiles, head))
    parts = swap(tiles, NEAR)
    hi = lax.ppermute(head_late, "gz", [(i + 1, i) for i in range(slabs - 1)])
    kernel = kernel_taps.reshape(27, cin, cout)
    ahead = kernel.reshape(27 * cin, cout).T
    back = kernel[::-1].reshape(3, 9, cin, cout).transpose(1, 2, 0, 3).reshape(9 * cin, 3 * cout)
    bias = channel_bias[:, None]
    part, ahead, back, bias = lax.optimization_barrier((jnp.sum(parts, axis=0), ahead, back, bias))
    planes = (lo, head, mid, tail, hi)
    output = forward(cin, planes, ahead, bias, part)
    grad_input = backward(cin, planes, back, part)
    far = lax.axis_size("dp_0")
    part = jnp.broadcast_to(part, (far, *part.shape))
    part = swap(part, "dp_0")
    part = jnp.sum(part, axis=0)
    part, output, grad_input = lax.optimization_barrier((part, output, grad_input))
    rounded = lax.reduce_precision(part, 8, 7)
    last = core * TILES + lax.axis_index(NEAR) >= BIAS_ROW // 8 * (cin // 2)
    rest = last & (lax.broadcasted_iota(jnp.int32, part.shape, 0) == (BIAS_ROW + 1) % 8)
    part = jnp.where(rest, part - rounded, rounded).astype(jnp.bfloat16)
    total = swap(jnp.broadcast_to(part, (2 * TILES, *part.shape)), (CORE, *NEAR)).astype(jnp.float32)
    total = total.reshape(4, 16, 8, 128).transpose(0, 2, 1, 3).reshape(ROWS, 2048)
    bias_total = total[BIAS_ROW, :cout] + total[BIAS_ROW + 1, :cout]
    return (output[None], grad_input[None], total[:27], bias_total)


def solution(mesh):
    split = Mesh(mesh.devices.reshape(16, 8, 2, mesh.shape["gz"]), ("dp_0", "dp_1", "dp_2", "gz"))
    placed = (P(DP, None, "gz", None), P(), P(), P(DP, None, "gz", None))
    return jax.shard_map(
        on_device,
        mesh=split,
        in_specs=placed,
        out_specs=(P(DP, None, "gz", None), P(DP, None, "gz", None), P(), P()),
        check_vma=False,
    )
```

```python
import functools
import math

import jax
import jax.numpy as jnp
from jax import lax
from jax.experimental import pallas as pl
from jax.experimental.pallas import tpu as pltpu
from jax.sharding import Mesh
from jax.sharding import PartitionSpec as P


NX = 64
NY = 8
DP = ("dp_0", "dp_1", "dp_2")
CORE = "dp_2"
NEAR = ("dp_1", "gz")
TILES = 32
ROWS = 32
BIAS_ROW = 27
INTERPRET = False
VMEM = pl.BlockSpec(memory_space=pltpu.VMEM)
SMEM = pl.BlockSpec(memory_space=pltpu.SMEM)


def on_core(body, out_shape, scratch=(), held=True, near=True):
    def call(*operands):
        if held:
            operands = [x if x.ndim == 1 else pltpu.with_memory_space_constraint(x, pltpu.VMEM) for x in operands]
        return pl.pallas_call(
            body,
            out_shape=jax.tree.map(lambda s: pltpu.VMEM(s.shape, s.dtype), out_shape) if near else out_shape,
            in_specs=[SMEM if x.ndim == 1 else VMEM for x in operands],
            out_specs=jax.tree.map(lambda _: VMEM, out_shape),
            scratch_shapes=list(scratch),
            interpret=INTERPRET,
        )(*operands)

    return call


def inside(width, db, dc):
    lane = lax.broadcasted_iota(jnp.int32, (1, width), 1)
    x = (lane & (NX - 1)) + dc
    y = lax.shift_right_logical(lane, NX.bit_length() - 1) + db
    return (x >= 0) & (x < NX) & (y >= 0) & (y < NY)


def moved(plane, b, c):
    width = plane.shape[-1]
    off = (b - 1) * NX + c - 1
    if off == 0:
        return plane
    return jnp.where(inside(width, b - 1, c - 1), pltpu.roll(plane, (-off) % width, 1), 0.0)


def store_moved(s_ref, at, plane):
    plane = plane.astype(jnp.float32)
    chans = plane.shape[0]
    for b in range(3):
        for c in range(3):
            row = at + (3 * b + c) * chans
            s_ref[row : row + chans, :] = moved(plane, b, c).astype(jnp.bfloat16)


def split_body(f_ref, u_ref, head_ref, mid_ref, tail_ref):
    cin, planes, _ = f_ref.shape
    for ref, at in ((f_ref, 0), (u_ref, cin)):
        rows = slice(at, at + ref.shape[0])
        own = jnp.swapaxes(ref[...].astype(jnp.float32), 0, 1).astype(jnp.bfloat16)
        head_ref[rows, :] = own[0]
        tail_ref[rows, :] = own[planes - 1]
        for z in range(1, planes - 1):
            mid_ref[z - 1, rows, :] = own[z]


def planes_of(head_ref, mid_ref, tail_ref, rows):
    mid = [mid_ref[z, rows, :] for z in range(mid_ref.shape[0])]
    return [head_ref[rows, :], *mid, tail_ref[rows, :]]


NT = (((1,), (1,)), ((), ()))


def dot(a, b, dims=(((1,), (0,)), ((), ()))):
    return lax.dot_general(a, b, dims, preferred_element_type=jnp.float32)


def own_body(cin, head_ref, mid_ref, tail_ref, w_ref, moved_ref, s_ref):
    width = head_ref.shape[1]
    cout = head_ref.shape[0] - cin
    taps = 9 * cin
    own = planes_of(head_ref, mid_ref, tail_ref, slice(0, cin))
    ups = planes_of(head_ref, mid_ref, tail_ref, slice(cin, cin + cout))
    planes = len(own)
    for z in range(planes):
        store_moved(s_ref, z * taps, own[z])
    moved_ref[...] = s_ref[:taps, :]
    twice = [jnp.concatenate([up, up], axis=0) for up in ups]
    for a in range(3):
        total = jnp.zeros((taps, 2 * cout), jnp.float32)
        for z in range(planes):
            src = z + a - 1
            if 0 <= src < planes:
                total += dot(s_ref[src * taps : (src + 1) * taps, :], twice[z], NT)
        w_ref[a * taps : (a + 1) * taps, :] = total
    ones = jnp.ones((16, width), jnp.bfloat16)
    bias = jnp.zeros((16, 2 * cout), jnp.float32)
    for z in range(planes):
        bias += dot(ones, twice[z], NT)
    w_ref[3 * taps :, :] = jnp.zeros((w_ref.shape[0] - 3 * taps, 2 * cout), jnp.float32)
    for row in (BIAS_ROW, BIAS_ROW + 1):
        w_ref[row * cin : row * cin + 8, :] = bias[:8]


def edge_body(cin, factor, core_ref, lo_ref, head_ref, moved_ref, w_ref, keep_ref, send_ref, s_ref, v_ref):
    cout = lo_ref.shape[0] - cin
    taps = 9 * cin
    v_ref[...] = w_ref[...]
    store_moved(s_ref, 0, lo_ref[:cin, :])
    for a, sources_ref, up in ((0, s_ref, head_ref[cin:, :]), (2, moved_ref, lo_ref[cin:, :])):
        twice = jnp.concatenate([up, up], axis=0)
        v_ref[a * taps : (a + 1) * taps, :] += dot(sources_ref[...], twice, NT)
    left = lax.broadcasted_iota(jnp.int32, (ROWS, 2 * cout), 1) < cout
    first = core_ref[0] == 0
    for at in range(cin // 2):
        even = v_ref[pl.ds(2 * at, ROWS, stride=cin), :]
        odd = v_ref[pl.ds(2 * at + 1, ROWS, stride=cin), :]
        both = (jnp.where(left, even, odd) * factor).reshape(2, ROWS // 16, 8, 2 * cout)
        keep_ref[:, at] = jnp.where(first, both[0], both[1])
        send_ref[:, at] = jnp.where(first, both[1], both[0])


def forward_body(cin, lo_ref, head_ref, mid_ref, tail_ref, hi_ref, w_ref, bias_ref, _, out_ref, s_ref):
    taps = 9 * cin
    rows = slice(0, cin)
    slabs = [lo_ref[rows, :], *planes_of(head_ref, mid_ref, tail_ref, rows), hi_ref[rows, :]]
    for z, plane in enumerate(slabs):
        store_moved(s_ref, z * taps, plane)
    outs = [dot(w_ref[...], s_ref[z * taps : (z + 3) * taps, :]) + bias_ref[...] for z in range(len(slabs) - 2)]
    out_ref[...] = jnp.swapaxes(jnp.stack(outs), 0, 1).astype(jnp.bfloat16)


def backward_body(cin, lo_ref, head_ref, mid_ref, tail_ref, hi_ref, w_ref, _, out_ref, p_ref):
    width = lo_ref.shape[1]
    cout = lo_ref.shape[0] - cin
    rows = slice(cin, cin + cout)
    slabs = [lo_ref[rows, :], *planes_of(head_ref, mid_ref, tail_ref, rows), hi_ref[rows, :]]
    for z, plane in enumerate(slabs):
        p_ref[z * cout : (z + 1) * cout, :] = plane
    outs = []
    for z in range(len(slabs) - 2):
        parts = dot(w_ref[...], p_ref[z * cout : (z + 3) * cout, :])
        total = jnp.zeros((cin, width), jnp.float32)
        for b in range(3):
            for c in range(3):
                at = (3 * b + c) * cin
                total += moved(parts[at : at + cin], b, c)
        outs.append(total)
    out_ref[...] = jnp.swapaxes(jnp.stack(outs), 0, 1).astype(jnp.bfloat16)


def split_planes(feats, grads):
    planes, width = feats.shape[1:]
    rows = feats.shape[0] + grads.shape[0]
    one = jax.ShapeDtypeStruct((rows, width), feats.dtype)
    mid = jax.ShapeDtypeStruct((planes - 2, rows, width), feats.dtype)
    return on_core(split_body, (one, mid, one), held=False)(feats, grads)


def own_terms(cin, head, mid, tail):
    rows, width = head.shape
    planes = mid.shape[0] + 2
    return on_core(
        functools.partial(own_body, cin),
        (jax.ShapeDtypeStruct((ROWS * cin, 2 * (rows - cin)), jnp.float32), jax.ShapeDtypeStruct((9 * cin, width), jnp.bfloat16)),
        [pltpu.VMEM((planes * 9 * cin, width), jnp.bfloat16)],
    )(head, mid, tail)


def weight_tiles(cin, core, lo, head, head_moved, own, factor):
    rows, width = lo.shape
    half = jax.ShapeDtypeStruct((ROWS // 16, cin // 2, 8, 2 * (rows - cin)), jnp.float32)
    return on_core(
        functools.partial(edge_body, cin, factor),
        (half, half),
        [pltpu.VMEM((9 * cin, width), jnp.bfloat16), pltpu.VMEM(own.shape, jnp.float32)],
    )(core, lo, head, head_moved, own)


def forward(cin, slabs, taps, bias, after):
    rows, width = slabs[0].shape
    planes = slabs[2].shape[0] + 2
    return on_core(
        functools.partial(forward_body, cin),
        jax.ShapeDtypeStruct((rows - cin, planes, width), jnp.bfloat16),
        [pltpu.VMEM(((planes + 2) * 9 * cin, width), jnp.bfloat16)],
        near=False,
    )(*slabs, taps, bias, after)


def backward(cin, slabs, taps, after):
    rows, width = slabs[0].shape
    planes = slabs[2].shape[0] + 2
    return on_core(
        functools.partial(backward_body, cin),
        jax.ShapeDtypeStruct((cin, planes, width), jnp.bfloat16),
        [pltpu.VMEM(((planes + 2) * (rows - cin), width), jnp.bfloat16)],
        near=False,
    )(*slabs, taps, after)


def swap(blocks, axes):
    return lax.all_to_all(blocks, axes, 0, 0, tiled=True)


def on_device(features_in, kernel_taps, channel_bias, upstream):
    feats, grads = features_in[0], upstream[0]
    cin, depth, width = feats.shape
    cout = grads.shape[0]
    cells_all = lax.axis_size(DP) * depth * lax.axis_size("gz") * width
    factor = 1.0 / math.sqrt(cells_all)
    head, mid, tail = split_planes(feats, grads)
    slabs = lax.axis_size("gz")
    lo = lax.ppermute(tail, "gz", [(i, i + 1) for i in range(slabs - 1)])
    hi = lax.ppermute(head, "gz", [(i + 1, i) for i in range(slabs - 1)])
    own, head_moved = own_terms(cin, head, mid, tail)
    core = lax.axis_index(CORE)
    keep, send = weight_tiles(cin, core[None], lo, head, head_moved, own, factor)
    other = lax.ppermute(send, CORE, [(0, 1), (1, 0)])
    tiles = (keep + other).reshape(TILES, 8, 128)
    parts = swap(tiles, NEAR)
    part, kernel_taps, channel_bias = lax.optimization_barrier((jnp.sum(parts, axis=0), kernel_taps, channel_bias))
    kernel = kernel_taps.reshape(27, cin, cout)
    ahead = kernel.reshape(27 * cin, cout).T
    back = kernel[::-1].reshape(3, 9, cin, cout).transpose(1, 2, 0, 3).reshape(9 * cin, 3 * cout)
    bias = channel_bias[:, None]
    planes = (lo, head, mid, tail, hi)
    output = forward(cin, planes, ahead, bias, part)
    grad_input = backward(cin, planes, back, part)
    far = lax.axis_size("dp_0")
    part = jnp.broadcast_to(part, (far, *part.shape))
    part = swap(part, "dp_0")
    part = jnp.sum(part, axis=0)
    part, output, grad_input = lax.optimization_barrier((part, output, grad_input))
    rounded = lax.reduce_precision(part, 8, 7)
    last = core * TILES + lax.axis_index(NEAR) >= BIAS_ROW // 8 * (cin // 2)
    rest = last & (lax.broadcasted_iota(jnp.int32, part.shape, 0) == (BIAS_ROW + 1) % 8)
    part = jnp.where(rest, part - rounded, rounded).astype(jnp.bfloat16)
    total = swap(jnp.broadcast_to(part, (2 * TILES, *part.shape)), (CORE, *NEAR)).astype(jnp.float32)
    total = total.reshape(4, 16, 8, 128).transpose(0, 2, 1, 3).reshape(ROWS, 2048)
    bias_total = total[BIAS_ROW, :cout] + total[BIAS_ROW + 1, :cout]
    return (output[None], grad_input[None], total[:27], bias_total)


def solution(mesh):
    split = Mesh(mesh.devices.reshape(16, 8, 2, mesh.shape["gz"]), ("dp_0", "dp_1", "dp_2", "gz"))
    placed = (P(DP, None, "gz", None), P(), P(), P(DP, None, "gz", None))
    return jax.shard_map(
        on_device,
        mesh=split,
        in_specs=placed,
        out_specs=(P(DP, None, "gz", None), P(DP, None, "gz", None), P(), P()),
        check_vma=False,
    )
```
